32 devices in a mesh: groups: 2 (over y), expert: 8 (over z, core), attn: 2 (over x).
Axes of the slice: x: 2, y: 2, z: 4, core: 2. Of those that a mesh axis runs over, the one named last changes fastest.
Arguments:
- tokens: bfloat16 [512, 3584], P(('groups', 'expert')), parts along dimension 0, may hold values from -6 to 6
- gates: float32 [512, 8], P(('groups', 'expert')), parts along dimension 0, may hold values from 0.05 to 0.6
- slots: int32 [512, 8], P(('groups', 'expert')), parts along dimension 0, may hold values from 0 to 15, all different within a row; in each aligned block of 32 rows (0 to 31, 32 to 63, ...) at most 20 rows name the same one
- plan: int32 [16], P('groups'), parts along dimension 0, may hold values from 0 to 7, as said below
- gate_proj: bfloat16 [8, 3584, 1024], P('expert', None, 'attn'), may hold values from -0.09375 to 0.09375
- up_proj: bfloat16 [8, 3584, 1024], P('expert', None, 'attn'), may hold values from -0.09375 to 0.09375
- down_proj: bfloat16 [8, 3584, 1024], P('expert', None, 'attn'), may hold values from -0.1875 to 0.1875
Outputs:
- moe_out: bfloat16 [512, 3584], P(('groups', 'expert')), parts along dimension 0
The draws below stay inside these ranges and needn't reach their ends.
There are 2 independent parts, one for each index of `groups`. The reference program is written for one: setup_inputs(seed, part) draws one part's arguments, and reference() takes and returns one part's arrays. A program takes and returns all parts, laid end to end along the dimension named above; an argument that names none is the same for every part. Nothing has to cross between parts.
Inputs may be any that keep to these rules, and one draw needn't show every extreme that they name: A row's 8 slots are distinct; among the 32 rows of one index of expert (aligned blocks) no slot is named more than 20 times, a bound that some block reaches. plan[d] is never d; no expert is named by more than 2 entries of plan, and some expert by exactly 2.
All inputs are finite; a program needn't handle non-finite values.
Results may differ from the reference program's by a relative error of at most 0.014.
Values may be sent and summed in bfloat16 or wider, within the bound.
A program may use at most 128 MiB of HBM per device.

```python
import math
import jax
import jax.numpy as jnp
import numpy as np
from jax import lax

D = 3584
FF = 1024
TOP = 8
TOK_DEV = 32
TOKENS = 256
EXPERTS = 8
SPARES = 8
SLOTS = 16
CAP = 20
N_EXPERT = 8
N_ATTN = 2


def draw_plan(key, part):
    order = jax.random.permutation(jax.random.fold_in(key, 11), SPARES).astype(jnp.int32)
    index = jnp.arange(SPARES, dtype=jnp.int32)
    half = SPARES // 2
    target = jnp.where(index < half, index // 2 * 2 + 2, (index + 1) % SPARES)
    result = jnp.zeros((SPARES,), jnp.int32).at[order].set(order[target])
    return result


def levels(stream_key, shape, shards, low, high):
    loudness = 1.0
    for axis_at, blocks in shards:
        draws = jax.random.uniform(jax.random.fold_in(jax.random.fold_in(stream_key, 6), axis_at), (blocks,), jnp.float32, low / len(shards), high / len(shards))
        loudness = loudness * jnp.repeat(jnp.exp(draws), shape[axis_at] // blocks).reshape((-1,) + (1,) * (len(shape) - 1 - axis_at))
    return loudness


def routed_block(rng, own, number, rows, count, top, limit, slope):
    order = jax.random.permutation(rng, count)
    packed, usual = portions_of(count, rows * top, limit, slope, True), portions_of(count, rows * top, limit, slope, False)
    places = jnp.arange(count)

    def named(lengths, rotation):
        used = int((lengths > 0).sum())
        fixed = max(1, used // 4)
        moved = fixed + (places - fixed + rotation * (used - fixed)) % max(1, count - fixed)
        return jnp.zeros((count,), jnp.int32).at[order[jnp.where(places < fixed, places, moved)]].set(jnp.asarray(lengths, jnp.int32))

    lengths = jnp.where(number % 4 == 0, named(packed, number // 4), named(usual, number - number // 4 - 1))
    mixed = jax.random.permutation(jax.random.fold_in(own, 3), count)
    giver, taker = mixed[0:count // 2 * 2:2], mixed[1:count // 2 * 2:2]
    margin = jnp.minimum(lengths[giver] - 1, limit - lengths[taker]) // 2
    margin = jnp.where((giver == order[0]) | (taker == order[0]) | (lengths[taker] == 0), 0, jnp.maximum(margin, 0))
    moved = jax.random.randint(jax.random.fold_in(own, 4), (count // 2,), 0, 1 << 20) % (margin + 1)
    lengths = lengths.at[giver].add(-moved).at[taker].add(moved)
    labels = jnp.searchsorted(jnp.cumsum(lengths), jnp.arange(rows * top), side="right").astype(jnp.int32)
    table = labels.reshape(top, rows).T
    table = table[jax.random.permutation(jax.random.fold_in(own, 1), rows)]
    rotation = jax.random.randint(jax.random.fold_in(own, 2), (rows, 1), 0, top)
    return jnp.take_along_axis(table, (jnp.arange(top)[None, :] + rotation) % top, axis=1)


def portions_of(amount, total, limit, skew, full):
    portions = [(1 << 20) // math.isqrt(grade ** skew) + 1 for grade in range(1, amount + 1)]
    largest = limit if full else min(limit, max(-(-total // amount), total * portions[0] // sum(portions)))
    least = 1 if total - largest >= amount - 1 else 0
    counts, spare = [largest] + [least] * (amount - 1), total - largest - least * (amount - 1)
    while spare > 0:
        free = [i for i in range(1, amount) if counts[i] < largest] or [i for i in range(1, amount) if counts[i] < limit]
        whole, budget = sum([portions[i] for i in free]), spare
        for i in free:
            more = min(limit - counts[i], max(1, budget * portions[i] // whole), spare)
            counts[i] = counts[i] + more
            spare = spare - more
    return np.array(counts)


def noise(key, extent, deviation, reach, pieces=(), kind=jnp.bfloat16):
    drawn = deviation * jax.random.normal(key, extent, jnp.float32)
    if pieces:
        drawn = drawn * levels(key, extent, pieces, -0.22, 0.18)
    return jnp.clip(drawn, -reach, reach).astype(kind)


def setup_inputs(seed: int = 0, part: int = 0) -> dict:
    streams_of = jax.random.split(jax.random.key(seed), 8)
    part_splits = jax.random.split(jax.random.fold_in(streams_of[7], part), 8)
    tokens = noise(part_splits[0], (TOKENS, D), 1.0, 6.0, ((0, 8),))
    gates = jnp.clip(jnp.exp(math.log(0.6) - 2.4849067 * jax.random.uniform(part_splits[1], (TOKENS, TOP), jnp.float32) ** levels(part_splits[1], (TOKENS, TOP), ((0, 8),), -0.2, 0.2)), 0.05, 0.6)
    slots_keys = jax.random.split(jax.random.fold_in(part_splits[2], 1), TOKENS // TOK_DEV)
    slots_turns = jax.random.permutation(jax.random.fold_in(part_splits[2], 3), TOKENS // TOK_DEV)
    slots = jax.vmap(lambda own, number: routed_block(jax.random.fold_in(part_splits[2], 2), own, number, TOK_DEV, SLOTS, TOP, CAP, 1))(slots_keys, slots_turns).reshape((TOKENS, TOP))
    plan = draw_plan(jax.random.fold_in(jax.random.fold_in(streams_of[7], part), 71), part)
    gate_proj = noise(streams_of[4], (EXPERTS, D, FF), D ** -0.5, 0.09375, ((0, 8), (2, 2)))
    up_proj = noise(streams_of[5], (EXPERTS, D, FF), D ** -0.5, 0.09375, ((0, 8), (2, 2)))
    down_proj = noise(streams_of[6], (EXPERTS, D, FF), FF ** -0.5, 0.1875, ((0, 8), (2, 2)))
    return dict(tokens=tokens, gates=gates, slots=slots, plan=plan, gate_proj=gate_proj, up_proj=up_proj, down_proj=down_proj)


def expert_rows(rows, w_gate, w_up, w_down):
    rows_float = rows.astype(jnp.float32)
    gate_act = jnp.dot(rows_float, w_gate.astype(jnp.float32), precision=lax.Precision.HIGHEST)
    up_act = jnp.dot(rows_float, w_up.astype(jnp.float32), precision=lax.Precision.HIGHEST)
    hidden = (jax.nn.silu(gate_act) * up_act).astype(jnp.bfloat16)
    row_count = rows.shape[0]
    group = FF // N_ATTN
    hidden_split = hidden.astype(jnp.float32).reshape(row_count, N_ATTN, group)
    down_split = w_down.astype(jnp.float32).reshape(D, N_ATTN, group)
    down_part = jnp.einsum("rap,dap->rad", hidden_split, down_split, precision=lax.Precision.HIGHEST)
    down_part = lax.optimization_barrier(down_part.astype(jnp.bfloat16))
    return jnp.sum(down_part.astype(jnp.float32), axis=1)


def reference(tokens, gates, slots, plan, gate_proj, up_proj, down_proj):
    slot_ids = jnp.arange(2 * N_EXPERT, dtype=jnp.int32)
    expert_of = jnp.where(slot_ids % 2 == 0, slot_ids // 2, plan[slot_ids // 2]).astype(jnp.int32)
    per_block = TOK_DEV * TOP
    pair_slots = slots.reshape(N_EXPERT, per_block).astype(jnp.int32)
    onehot = (pair_slots[:, :, None] == slot_ids[None, None, :]).astype(jnp.int32)
    running = jnp.cumsum(onehot, axis=1)
    position = (jnp.sum(running * onehot, axis=2) - 1).astype(jnp.int32)
    block_index = jnp.broadcast_to(jnp.arange(N_EXPERT, dtype=jnp.int32)[:, None], (N_EXPERT, per_block))
    local_token = jnp.broadcast_to((jnp.arange(per_block, dtype=jnp.int32) // TOP)[None, :], (N_EXPERT, per_block))
    token_table = jnp.zeros((2 * N_EXPERT, N_EXPERT, CAP), jnp.int32)
    token_table = token_table.at[pair_slots, block_index, position].set(local_token + block_index * TOK_DEV)

    def one_slot(slot):
        expert = expert_of[slot]
        rows = tokens[token_table[slot].reshape(-1)]
        result = expert_rows(rows, gate_proj[expert], up_proj[expert], down_proj[expert])
        return result.reshape(N_EXPERT, CAP, D)

    outputs = lax.map(one_slot, slot_ids)
    picked = outputs[pair_slots, block_index, position]
    picked = picked.reshape(N_EXPERT * TOK_DEV, TOP, D)
    total = jnp.sum(picked * gates[:, :, None], axis=1)
    return total.astype(jnp.bfloat16)
```

```python
import functools

import jax
import jax.numpy as jnp
from jax import lax
from jax.experimental import pallas as pl
from jax.experimental.pallas import tpu as pltpu
from jax.sharding import PartitionSpec as P

MESH = pl.DeviceIdType.MESH
LANES = 128
LAG = 3


def combined_gates(gates, slots, plan, experts):
    choice = slots // 2
    expert = jnp.where(slots % 2 == 0, choice, plan[choice])
    ids = jnp.arange(experts, dtype=jnp.int32)
    return jnp.sum(jnp.where(expert[:, :, None] == ids, gates[:, :, None], 0.0), axis=1)


def dense_body(tokens, gates, slots, plan, gate_proj, up_proj, down_proj):
    experts = lax.axis_size("expert")
    weight = combined_gates(gates, slots, plan, experts)
    everyone = lax.all_gather(tokens, "expert", axis=0, tiled=True)
    weights = lax.all_to_all(weight, "expert", split_axis=1, concat_axis=0, tiled=True)
    gate_act = jnp.dot(everyone, gate_proj[0], preferred_element_type=jnp.float32)
    up_act = jnp.dot(everyone, up_proj[0], preferred_element_type=jnp.float32)
    hidden = (jax.nn.silu(gate_act) * up_act).astype(jnp.bfloat16)
    down = jnp.einsum("rf,df->rd", hidden, down_proj[0], preferred_element_type=jnp.float32)
    part = (down * weights).astype(jnp.bfloat16)
    part = lax.psum_scatter(part, "expert", scatter_dimension=0, tiled=True)
    return lax.psum(part, "attn")


def kernel(
    nz, steps, width,
    tokens, gates, slots, plan, gate_hbm, up_hbm, down_hbm,
    out,
    rows, wg, wu, wd, hid, scale, grow_send, grow,
    keep, a_send, a_recv, b_send, b_recv, c_send, c_recv, d_send,
    send_sem, local_sem, row_sem, g_sem, a_sem, b_sem, c_sem, d_sem,
):
    f32, bf16 = jnp.float32, jnp.bfloat16
    experts = 2 * nz
    me = lax.axis_index("expert")
    x = lax.axis_index("attn")
    z, c = me // 2, me % 2
    half = rows.shape[-1]
    tok = rows.shape[-2]
    mine = pl.ds(pl.multiple_of(x * half, LANES), half)
    other = pl.ds(pl.multiple_of((1 - x) * half, LANES), half)
    partner = {"expert": z * 2 + (1 - c)}
    across = {"attn": 1 - x}

    counts = {"send": 0, "local": 0}
    pending = []

    def local(src, dst):
        copy = pltpu.make_async_copy(src, dst, local_sem.at[counts["local"]])
        counts["local"] += 1
        copy.start()
        return copy

    def send(src, dst, sem, device, when=None):
        copy = pltpu.make_async_remote_copy(
            src_ref=src, dst_ref=dst, send_sem=send_sem.at[counts["send"]], recv_sem=sem,
            device_id=device, device_id_type=MESH,
        )
        counts["send"] += 1
        if when is None:
            copy.start()
        else:
            pl.when(when)(copy.start)
        pending.append((when, copy))

    def arrived(dst, sem):
        pltpu.make_async_remote_copy(
            src_ref=dst, dst_ref=dst, send_sem=send_sem.at[0], recv_sem=sem,
            device_id=partner, device_id_type=MESH,
        ).wait_recv()

    own_copies = [
        local(tokens.at[:, mine], rows.at[0, 0, z]),
        local(tokens.at[:, other], rows.at[1, 0, z]),
    ]
    weight_copies = []
    for h, part in enumerate((mine, other)):
        weight_copies.append(local(gate_hbm.at[0, part, :], wg.at[h]))
        weight_copies.append(local(up_hbm.at[0, part, :], wu.at[h]))
    down_copies = [local(down_hbm.at[0, other, :], wd.at[1]), local(down_hbm.at[0, mine, :], wd.at[0])]

    barrier = pltpu.get_barrier_semaphore()
    for dz in range(nz):
        for r in range(2):
            if dz or r:
                peer = {"expert": ((z + dz) % nz) * 2 + (c if r == 0 else 1 - c)}
                pl.semaphore_signal(barrier, inc=1, device_id=peer, device_id_type=MESH)
    pl.semaphore_signal(barrier, inc=1, device_id=across, device_id_type=MESH)

    diagonal = lax.broadcasted_iota(jnp.int32, (tok, LANES), 0) == lax.broadcasted_iota(
        jnp.int32, (tok, LANES), 1
    )
    named = slots[...]
    expert = lax.shift_right_logical(named, 1)
    target = expert
    for d in range(experts):
        target = jnp.where(expert == d, plan[d], target)
    expert = jnp.where((named & 1) == 0, expert, target)
    gate = gates[...]
    for e in range(experts):
        column = jnp.sum(jnp.where(expert == e, gate, 0.0), axis=1, keepdims=True)
        grow_send[e] = jnp.sum(jnp.where(diagonal, column, 0.0), axis=0, keepdims=True)

    pl.semaphore_wait(barrier, experts)

    for step in (1, -1):
        send(
            tokens.at[:, mine], rows.at[0, 0, z], row_sem.at[0, 0, z],
            {"expert": (z + step) * 2 + c}, (z + step >= 0) & (z + step < nz),
        )
    send(tokens.at[:, mine], rows.at[0, 1, z], row_sem.at[0, 1, z], partner)
    send(tokens.at[:, other], rows.at[1, 1, z], row_sem.at[1, 1, z], partner)
    for dz in range(nz):
        for r in range(2):
            if dz or r:
                peer = ((z + dz) % nz) * 2 + (c if r == 0 else 1 - c)
                send(grow_send.at[peer], grow.at[r, z], g_sem.at[r, z], {"expert": peer})
    grow[0, z] = grow_send[me]

    for hop in range(1, nz + 1):
        for step in (1, -1):
            if hop < nz:
                origin = z - step * hop
                valid = (origin >= 0) & (origin < nz)
                slot = jnp.clip(origin, 0, nz - 1)
                block = rows.at[0, 0, slot]
                pl.when(valid)(functools.partial(arrived, block, row_sem.at[0, 0, slot]))
                if hop < nz - 1:
                    send(
                        block, block, row_sem.at[0, 0, slot], {"expert": (z + step) * 2 + c},
                        valid & (z + step >= 0) & (z + step < nz),
                    )
                send(block, rows.at[1, 0, slot], row_sem.at[1, 0, slot], across, valid)
                send(block, rows.at[0, 1, slot], row_sem.at[0, 1, slot], partner, valid)
        for step in (1, -1):
            if hop > 1:
                origin = z - step * (hop - 1)
                valid = (origin >= 0) & (origin < nz)
                slot = jnp.clip(origin, 0, nz - 1)
                block = rows.at[1, 0, slot]
                pl.when(valid)(functools.partial(arrived, block, row_sem.at[1, 0, slot]))
                send(block, rows.at[1, 1, slot], row_sem.at[1, 1, slot], partner, valid)

    for dz in range(nz):
        for r in range(2):
            if dz or r:
                slot = (z + dz) % nz
                arrived(grow.at[r, slot], g_sem.at[r, slot])
    for r in range(2):
        for i in range(nz):
            column = jnp.sum(jnp.where(diagonal, grow[r, i], 0.0), axis=1, keepdims=True)
            scale[r, i] = jnp.broadcast_to(column, (tok, width))
    for copy in own_copies + weight_copies:
        copy.wait()
    for dz in range(nz):
        slot = (z + dz) % nz
        for h in range(2):
            arrived(rows.at[h, 1, slot], row_sem.at[h, 1, slot])

    total = 2 * nz * tok
    units = wg.shape[-1]
    tile = 256 if units % 256 == 0 else LANES
    for t in range(units // tile):
        cols = pl.ds(t * tile, tile)
        gate_act = up_act = None
        for h in range(2):
            block = rows[h].reshape(total, half)
            g = jnp.dot(block, wg[h, :, cols], preferred_element_type=f32)
            u = jnp.dot(block, wu[h, :, cols], preferred_element_type=f32)
            gate_act = g if gate_act is None else gate_act + g
            up_act = u if up_act is None else up_act + u
        hid[:, cols] = (gate_act / (1.0 + jnp.exp(-gate_act)) * up_act).astype(bf16)

    for copy in down_copies:
        copy.wait()

    def cross(j):
        arrived(a_recv.at[1, j], a_sem.at[1, j])
        b_send[j] = (keep[1, j] + a_recv[1, j].astype(f32)).astype(bf16)
        send(b_send.at[j], b_recv.at[j], b_sem.at[j], across)

    for j in range(steps):
        for h in (1, 0):
            down = lax.dot_general(
                hid[...], wd[h, pl.ds(j * width, width), :], (((1,), (1,)), ((), ())),
                preferred_element_type=f32,
            )
            down = down.reshape(2, nz, tok, width) * scale[...]
            a_send[h, j] = down[1].astype(bf16)
            keep[h, j] = down[0]
            send(a_send.at[h, j], a_recv.at[h, j], a_sem.at[h, j], partner)
        if j:
            cross(j - 1)
    cross(steps - 1)

    out_copies = []

    def finish(j):
        value = keep[0, j, z] + a_recv[0, j, z].astype(f32) + b_recv[j, z].astype(f32)
        for d in range(nz - 1):
            arrived(c_recv.at[j, d], c_sem.at[j, d])
        for d in range(nz - 1):
            value = value + c_recv[j, d].astype(f32)
        d_send[j] = value.astype(bf16)
        cols = pl.ds(pl.multiple_of(x * half + j * width, LANES), width)
        send(d_send.at[j], out.at[:, cols], d_sem.at[j], across)
        out_copies.append(local(d_send.at[j], out.at[:, cols]))

    for j in range(steps + LAG):
        if j < steps:
            arrived(a_recv.at[0, j], a_sem.at[0, j])
            arrived(b_recv.at[j], b_sem.at[j])
            c_send[j] = (keep[0, j] + a_recv[0, j].astype(f32) + b_recv[j].astype(f32)).astype(bf16)
            for d in range(nz - 1):
                peer = (z + d + 1) % nz
                send(
                    c_send.at[j, peer], c_recv.at[j, d], c_sem.at[j, d], {"expert": peer * 2 + c}
                )
        if j >= LAG:
            finish(j - LAG)

    for j in range(steps):
        cols = pl.ds(pl.multiple_of((1 - x) * half + j * width, LANES), width)
        arrived(out.at[:, cols], d_sem.at[j])
    for copy in out_copies:
        copy.wait()
    for when, copy in pending:
        if when is None:
            copy.wait_send()
        else:
            pl.when(when)(copy.wait_send)


def fused_body(tokens, gates, slots, plan, gate_proj, up_proj, down_proj):
    f32, bf16 = jnp.float32, jnp.bfloat16
    nz = lax.axis_size("expert") // 2
    tok, model = tokens.shape
    half = model // 2
    units = gate_proj.shape[2]
    width = 256 if half % 256 == 0 else LANES
    steps = half // width
    dma = pltpu.SemaphoreType.DMA
    vmem, anywhere = pl.BlockSpec(memory_space=pltpu.VMEM), pl.BlockSpec(memory_space=pl.ANY)
    sends = 4 + 2 * nz + 8 * nz + steps * (3 + nz) + 4
    return pl.pallas_call(
        functools.partial(kernel, nz, steps, width),
        out_shape=jax.ShapeDtypeStruct((tok, model), bf16),
        in_specs=[
            anywhere, vmem, vmem, pl.BlockSpec(memory_space=pltpu.SMEM),
            anywhere, anywhere, anywhere,
        ],
        out_specs=anywhere,
        scratch_shapes=[
            pltpu.VMEM((2, 2, nz, tok, half), bf16),
            pltpu.VMEM((2, half, units), bf16),
            pltpu.VMEM((2, half, units), bf16),
            pltpu.VMEM((2, half, units), bf16),
            pltpu.VMEM((2 * nz * tok, units), bf16),
            pltpu.VMEM((2, nz, tok, width), f32),
            pltpu.VMEM((2 * nz, 1, LANES), f32),
            pltpu.VMEM((2, nz, 1, LANES), f32),
            pltpu.VMEM((2, steps, nz, tok, width), f32),
            pltpu.VMEM((2, steps, nz, tok, width), bf16),
            pltpu.VMEM((2, steps, nz, tok, width), bf16),
            pltpu.VMEM((steps, nz, tok, width), bf16),
            pltpu.VMEM((steps, nz, tok, width), bf16),
            pltpu.VMEM((steps, nz, tok, width), bf16),
            pltpu.VMEM((steps, nz - 1, tok, width), bf16),
            pltpu.VMEM((steps, tok, width), bf16),
            dma((sends,)),
            dma((8 + steps,)),
            dma((2, 2, nz)),
            dma((2, nz)),
            dma((2, steps)),
            dma((steps,)),
            dma((steps, nz - 1)),
            dma((steps,)),
        ],
        compiler_params=pltpu.CompilerParams(
            collective_id=0, has_side_effects=True, vmem_limit_bytes=48 * 1024 * 1024
        ),
    )(tokens, gates, slots, plan, gate_proj, up_proj, down_proj)


def body(tokens, gates, slots, plan, gate_proj, up_proj, down_proj):
    experts, attn = lax.axis_size("expert"), lax.axis_size("attn")
    tok, model = tokens.shape
    fits = (
        attn == 2 and experts % 2 == 0 and experts > 2
        and tok % 16 == 0 and tok <= LANES
        and model % (2 * LANES) == 0 and gate_proj.shape[0] == 1
        and gate_proj.shape[2] % LANES == 0
    )
    chosen = fused_body if fits else dense_body
    return chosen(tokens, gates, slots, plan, gate_proj, up_proj, down_proj)


def solution(mesh):
    return jax.shard_map(
        body,
        mesh=mesh,
        in_specs=(
            P(("groups", "expert"), None),
            P(("groups", "expert"), None),
            P(("groups", "expert"), None),
            P("groups"),
            P("expert", None, "attn"),
            P("expert", None, "attn"),
            P("expert", None, "attn"),
        ),
        out_specs=P(("groups", "expert"), None),
        check_vma=False,
    )
```

```python
import functools

import jax
import jax.numpy as jnp
from jax import lax
from jax.experimental import pallas as pl
from jax.experimental.pallas import tpu as pltpu
from jax.sharding import PartitionSpec as P

MESH = pl.DeviceIdType.MESH
LANES = 128
LAG = 3
ROWS = 16


def combined_gates(gates, slots, plan, experts):
    choice = slots // 2
    expert = jnp.where(slots % 2 == 0, choice, plan[choice])
    ids = jnp.arange(experts, dtype=jnp.int32)
    return jnp.sum(jnp.where(expert[:, :, None] == ids, gates[:, :, None], 0.0), axis=1)


def dense_body(tokens, gates, slots, plan, gate_proj, up_proj, down_proj):
    experts = lax.axis_size("expert")
    weight = combined_gates(gates, slots, plan, experts)
    everyone = lax.all_gather(tokens, "expert", axis=0, tiled=True)
    weights = lax.all_to_all(weight, "expert", split_axis=1, concat_axis=0, tiled=True)
    gate_act = jnp.dot(everyone, gate_proj[0], preferred_element_type=jnp.float32)
    up_act = jnp.dot(everyone, up_proj[0], preferred_element_type=jnp.float32)
    hidden = (jax.nn.silu(gate_act) * up_act).astype(jnp.bfloat16)
    down = jnp.einsum("rf,df->rd", hidden, down_proj[0], preferred_element_type=jnp.float32)
    part = (down * weights).astype(jnp.bfloat16)
    part = lax.psum_scatter(part, "expert", scatter_dimension=0, tiled=True)
    return lax.psum(part, "attn")


def kernel(
    nz, steps, width,
    tokens, gates, slots, plan, gate_hbm, up_hbm, down_hbm,
    out,
    rows, wg, wu, wd, acc, hid, scale, grow_send, grow,
    keep, a_send, a_recv, b_send, b_recv, c_send, c_recv, d_send,
    send_sem, local_sem, row_sem, g_sem, a_sem, b_sem, c_sem, d_sem,
):
    f32, bf16 = jnp.float32, jnp.bfloat16
    experts = 2 * nz
    me = lax.axis_index("expert")
    x = lax.axis_index("attn")
    z, c = me // 2, me % 2
    half = rows.shape[-1]
    tok = rows.shape[-2]
    mine = pl.ds(pl.multiple_of(x * half, LANES), half)
    other = pl.ds(pl.multiple_of((1 - x) * half, LANES), half)
    partner = {"expert": z * 2 + (1 - c)}
    across = {"attn": 1 - x}

    counts = {"send": 0, "local": 0}
    pending = []

    def local(src, dst):
        copy = pltpu.make_async_copy(src, dst, local_sem.at[counts["local"]])
        counts["local"] += 1
        copy.start()
        return copy

    def send(src, dst, sem, device, when=None):
        copy = pltpu.make_async_remote_copy(
            src_ref=src, dst_ref=dst, send_sem=send_sem.at[counts["send"]], recv_sem=sem,
            device_id=device, device_id_type=MESH,
        )
        counts["send"] += 1
        if when is None:
            copy.start()
        else:
            pl.when(when)(copy.start)
        pending.append((when, copy))

    def arrived(dst, sem):
        pltpu.make_async_remote_copy(
            src_ref=dst, dst_ref=dst, send_sem=send_sem.at[0], recv_sem=sem,
            device_id=partner, device_id_type=MESH,
        ).wait_recv()

    own_copies = [
        local(tokens.at[:, mine], rows.at[0, 0, z]),
        local(tokens.at[:, other], rows.at[1, 0, z]),
    ]
    weight_copies = []
    for h, part in enumerate((mine, other)):
        weight_copies.append(local(gate_hbm.at[0, part, :], wg.at[h]))
        weight_copies.append(local(up_hbm.at[0, part, :], wu.at[h]))
    down_copies = [local(down_hbm.at[0, other, :], wd.at[1]), local(down_hbm.at[0, mine, :], wd.at[0])]

    barrier = pltpu.get_barrier_semaphore()
    for dz in range(nz):
        for r in range(2):
            if dz or r:
                peer = {"expert": ((z + dz) % nz) * 2 + (c if r == 0 else 1 - c)}
                pl.semaphore_signal(barrier, inc=1, device_id=peer, device_id_type=MESH)
    pl.semaphore_signal(barrier, inc=1, device_id=across, device_id_type=MESH)

    diagonal = lax.broadcasted_iota(jnp.int32, (tok, LANES), 0) == lax.broadcasted_iota(
        jnp.int32, (tok, LANES), 1
    )
    named = slots[...]
    expert = lax.shift_right_logical(named, 1)
    target = expert
    for d in range(experts):
        target = jnp.where(expert == d, plan[d], target)
    expert = jnp.where((named & 1) == 0, expert, target)
    gate = gates[...]
    grow_send[...] = jnp.zeros_like(grow_send)
    for e in range(experts):
        grow_send[e, :, :tok] = jnp.sum(jnp.where(expert == e, gate, 0.0), axis=0, keepdims=True)

    pl.semaphore_wait(barrier, experts)

    pieces = tok // ROWS
    cuts = [pl.ds(q * ROWS, ROWS) for q in range(pieces)]

    def piece(h, r, slot, q):
        return rows.at[h, r, slot, cuts[q]], row_sem.at[h, r, slot, q]

    for q in range(pieces):
        for step in (1, -1):
            send(
                tokens.at[cuts[q], mine], *piece(0, 0, z, q),
                {"expert": (z + step) * 2 + c}, (z + step >= 0) & (z + step < nz),
            )
    for h, part in enumerate((mine, other)):
        for q in range(pieces):
            send(tokens.at[cuts[q], part], *piece(h, 1, z, q), partner)
    for dz in range(nz):
        for r in range(2):
            if dz or r:
                peer = ((z + dz) % nz) * 2 + (c if r == 0 else 1 - c)
                send(grow_send.at[peer], grow.at[r, z], g_sem.at[r, z], {"expert": peer})
    grow[0, z] = grow_send[me]

    items = [(hop, q) for hop in range(1, nz) for q in range(pieces)]

    def from_z(hop, q):
        for step in (1, -1):
            origin = z - step * hop
            valid = (origin >= 0) & (origin < nz)
            slot = jnp.clip(origin, 0, nz - 1)
            block, sem = piece(0, 0, slot, q)
            pl.when(valid)(functools.partial(arrived, block, sem))
            if hop < nz - 1:
                send(
                    block, block, sem, {"expert": (z + step) * 2 + c},
                    valid & (z + step >= 0) & (z + step < nz),
                )
            send(block, *piece(1, 0, slot, q), across, valid)
            send(block, *piece(0, 1, slot, q), partner, valid)

    def from_across(hop, q):
        for step in (1, -1):
            origin = z - step * hop
            valid = (origin >= 0) & (origin < nz)
            slot = jnp.clip(origin, 0, nz - 1)
            block, sem = piece(1, 0, slot, q)
            pl.when(valid)(functools.partial(arrived, block, sem))
            send(block, *piece(1, 1, slot, q), partner, valid)

    def from_partner(h):
        for dz in range(nz):
            for q in range(pieces):
                arrived(*piece(h, 1, (z + dz) % nz, q))

    total = 2 * nz * tok
    units = wg.shape[-1]
    tile = 256 if units % 256 == 0 else LANES
    tiles = [pl.ds(t * tile, tile) for t in range(units // tile)]

    def product(h, weights, cols):
        return jnp.dot(
            rows[h].reshape(total, half), weights[h, :, cols], preferred_element_type=f32
        )

    late = 2
    for i, item in enumerate(items):
        from_z(*item)
        if i >= late:
            from_across(*items[i - late])

    for copy in own_copies + weight_copies[:2]:
        copy.wait()
    from_partner(0)
    rest = list(items[-late:])
    for cols in tiles:
        acc[0, :, cols] = product(0, wg, cols)
        acc[1, :, cols] = product(0, wu, cols)
        if rest:
            from_across(*rest.pop(0))
    for item in rest:
        from_across(*item)

    for dz in range(nz):
        for r in range(2):
            if dz or r:
                slot = (z + dz) % nz
                arrived(grow.at[r, slot], g_sem.at[r, slot])
    for r in range(2):
        for i in range(nz):
            column = jnp.sum(jnp.where(diagonal, grow[r, i], 0.0), axis=1, keepdims=True)
            scale[r, i] = jnp.broadcast_to(column, (tok, width))
    for copy in weight_copies[2:]:
        copy.wait()
    from_partner(1)
    for cols in tiles:
        gate_act = acc[0, :, cols] + product(1, wg, cols)
        up_act = acc[1, :, cols] + product(1, wu, cols)
        hid[:, cols] = (gate_act / (1.0 + jnp.exp(-gate_act)) * up_act).astype(bf16)

    for copy in down_copies:
        copy.wait()

    def cross(j):
        arrived(a_recv.at[1, j], a_sem.at[1, j])
        b_send[j] = (keep[1, j] + a_recv[1, j].astype(f32)).astype(bf16)
        send(b_send.at[j], b_recv.at[j], b_sem.at[j], across)

    for j in range(steps):
        for h in (1, 0):
            down = lax.dot_general(
                hid[...], wd[h, pl.ds(j * width, width), :], (((1,), (1,)), ((), ())),
                preferred_element_type=f32,
            )
            down = down.reshape(2, nz, tok, width) * scale[...]
            a_send[h, j] = down[1].astype(bf16)
            keep[h, j] = down[0]
            send(a_send.at[h, j], a_recv.at[h, j], a_sem.at[h, j], partner)
        if j:
            cross(j - 1)
    cross(steps - 1)

    out_copies = []

    def finish(j):
        value = keep[0, j, z] + a_recv[0, j, z].astype(f32) + b_recv[j, z].astype(f32)
        for d in range(nz - 1):
            arrived(c_recv.at[j, d], c_sem.at[j, d])
        for d in range(nz - 1):
            value = value + c_recv[j, d].astype(f32)
        d_send[j] = value.astype(bf16)
        cols = pl.ds(pl.multiple_of(x * half + j * width, LANES), width)
        send(d_send.at[j], out.at[:, cols], d_sem.at[j], across)
        out_copies.append(local(d_send.at[j], out.at[:, cols]))

    for j in range(steps + LAG):
        if j < steps:
            arrived(a_recv.at[0, j], a_sem.at[0, j])
            arrived(b_recv.at[j], b_sem.at[j])
            c_send[j] = (keep[0, j] + a_recv[0, j].astype(f32) + b_recv[j].astype(f32)).astype(bf16)
            for d in range(nz - 1):
                peer = (z + d + 1) % nz
                send(
                    c_send.at[j, peer], c_recv.at[j, d], c_sem.at[j, d], {"expert": peer * 2 + c}
                )
        if j >= LAG:
            finish(j - LAG)

    for j in range(steps):
        cols = pl.ds(pl.multiple_of((1 - x) * half + j * width, LANES), width)
        arrived(out.at[:, cols], d_sem.at[j])
    for copy in out_copies:
        copy.wait()
    for when, copy in pending:
        if when is None:
            copy.wait_send()
        else:
            pl.when(when)(copy.wait_send)


def fused_body(tokens, gates, slots, plan, gate_proj, up_proj, down_proj):
    f32, bf16 = jnp.float32, jnp.bfloat16
    nz = lax.axis_size("expert") // 2
    tok, model = tokens.shape
    half = model // 2
    units = gate_proj.shape[2]
    width = 256 if half % 256 == 0 else LANES
    steps = half // width
    dma = pltpu.SemaphoreType.DMA
    vmem, anywhere = pl.BlockSpec(memory_space=pltpu.VMEM), pl.BlockSpec(memory_space=pl.ANY)
    sends = 2 * nz + (4 + 8 * nz) * (tok // ROWS) + steps * (3 + nz)
    return pl.pallas_call(
        functools.partial(kernel, nz, steps, width),
        out_shape=jax.ShapeDtypeStruct((tok, model), bf16),
        in_specs=[
            anywhere, vmem, vmem, pl.BlockSpec(memory_space=pltpu.SMEM),
            anywhere, anywhere, anywhere,
        ],
        out_specs=anywhere,
        scratch_shapes=[
            pltpu.VMEM((2, 2, nz, tok, half), bf16),
            pltpu.VMEM((2, half, units), bf16),
            pltpu.VMEM((2, half, units), bf16),
            pltpu.VMEM((2, half, units), bf16),
            pltpu.VMEM((2, 2 * nz * tok, units), f32),
            pltpu.VMEM((2 * nz * tok, units), bf16),
            pltpu.VMEM((2, nz, tok, width), f32),
            pltpu.VMEM((2 * nz, 1, LANES), f32),
            pltpu.VMEM((2, nz, 1, LANES), f32),
            pltpu.VMEM((2, steps, nz, tok, width), f32),
            pltpu.VMEM((2, steps, nz, tok, width), bf16),
            pltpu.VMEM((2, steps, nz, tok, width), bf16),
            pltpu.VMEM((steps, nz, tok, width), bf16),
            pltpu.VMEM((steps, nz, tok, width), bf16),
            pltpu.VMEM((steps, nz, tok, width), bf16),
            pltpu.VMEM((steps, nz - 1, tok, width), bf16),
            pltpu.VMEM((steps, tok, width), bf16),
            dma((sends,)),
            dma((8 + steps,)),
            dma((2, 2, nz, tok // ROWS)),
            dma((2, nz)),
            dma((2, steps)),
            dma((steps,)),
            dma((steps, nz - 1)),
            dma((steps,)),
        ],
        compiler_params=pltpu.CompilerParams(collective_id=0, has_side_effects=True),
    )(tokens, gates.T, slots.T, plan, gate_proj, up_proj, down_proj)


def body(tokens, gates, slots, plan, gate_proj, up_proj, down_proj):
    experts, attn = lax.axis_size("expert"), lax.axis_size("attn")
    tok, model = tokens.shape
    fits = (
        attn == 2 and experts % 2 == 0 and experts > 2
        and tok % ROWS == 0 and tok <= LANES
        and model % (2 * LANES) == 0 and gate_proj.shape[0] == 1
        and gate_proj.shape[2] % LANES == 0
    )
    chosen = fused_body if fits else dense_body
    return chosen(tokens, gates, slots, plan, gate_proj, up_proj, down_proj)


def solution(mesh):
    return jax.shard_map(
        body,
        mesh=mesh,
        in_specs=(
            P(("groups", "expert"), None),
            P(("groups", "expert"), None),
            P(("groups", "expert"), None),
            P("groups"),
            P("expert", None, "attn"),
            P("expert", None, "attn"),
            P("expert", None, "attn"),
        ),
        out_specs=P(("groups", "expert"), None),
        check_vma=False,
    )
```

```python
import functools

import jax
import jax.numpy as jnp
from jax import lax
from jax.experimental import pallas as pl
from jax.experimental.pallas import tpu as pltpu
from jax.sharding import PartitionSpec as P

MESH = pl.DeviceIdType.MESH
LANES = 128
LAG = 5
ROWS = 16
Z_FIRST = 2


def combined_gates(gates, slots, plan, experts):
    choice = slots // 2
    expert = jnp.where(slots % 2 == 0, choice, plan[choice])
    ids = jnp.arange(experts, dtype=jnp.int32)
    return jnp.sum(jnp.where(expert[:, :, None] == ids, gates[:, :, None], 0.0), axis=1)


def dense_body(tokens, gates, slots, plan, gate_proj, up_proj, down_proj):
    experts = lax.axis_size("expert")
    weight = combined_gates(gates, slots, plan, experts)
    everyone = lax.all_gather(tokens, "expert", axis=0, tiled=True)
    weights = lax.all_to_all(weight, "expert", split_axis=1, concat_axis=0, tiled=True)
    gate_act = jnp.dot(everyone, gate_proj[0], preferred_element_type=jnp.float32)
    up_act = jnp.dot(everyone, up_proj[0], preferred_element_type=jnp.float32)
    hidden = (jax.nn.silu(gate_act) * up_act).astype(jnp.bfloat16)
    down = jnp.einsum("rf,df->rd", hidden, down_proj[0], preferred_element_type=jnp.float32)
    part = (down * weights).astype(jnp.bfloat16)
    part = lax.psum_scatter(part, "expert", scatter_dimension=0, tiled=True)
    return lax.psum(part, "attn")


def kernel(
    nz, steps, width, z_first,
    tokens, gates, slots, plan, gate_hbm, up_hbm, down_hbm,
    out,
    rows, wg, wu, wd, acc, hid, scale, grow_send, grow,
    keep, a_send, a_recv, b_send, b_recv, c_send, c_recv, d_send,
    zc_send, zc_recv, e_send, e_recv, e_out,
    send_sem, local_sem, row_sem, g_sem, a_sem, b_sem, c_sem, d_sem, zc_sem, e_sem,
):
    f32, bf16 = jnp.float32, jnp.bfloat16
    experts = 2 * nz
    me = lax.axis_index("expert")
    x = lax.axis_index("attn")
    z, c = me // 2, me % 2
    half = rows.shape[-1]
    tok = rows.shape[-2]
    mine = pl.ds(pl.multiple_of(x * half, LANES), half)
    other = pl.ds(pl.multiple_of((1 - x) * half, LANES), half)
    partner = {"expert": z * 2 + (1 - c)}
    across = {"attn": 1 - x}

    counts = {"send": 0, "local": 0}
    pending = []

    def local(src, dst):
        copy = pltpu.make_async_copy(src, dst, local_sem.at[counts["local"]])
        counts["local"] += 1
        copy.start()
        return copy

    def send(src, dst, sem, device, when=None):
        copy = pltpu.make_async_remote_copy(
            src_ref=src, dst_ref=dst, send_sem=send_sem.at[counts["send"]], recv_sem=sem,
            device_id=device, device_id_type=MESH,
        )
        counts["send"] += 1
        if when is None:
            copy.start()
        else:
            pl.when(when)(copy.start)
        pending.append((when, copy))

    def arrived(dst, sem):
        pltpu.make_async_remote_copy(
            src_ref=dst, dst_ref=dst, send_sem=send_sem.at[0], recv_sem=sem,
            device_id=partner, device_id_type=MESH,
        ).wait_recv()

    own_copies = [
        local(tokens.at[:, mine], rows.at[0, 0, z]),
        local(tokens.at[:, other], rows.at[1, 0, z]),
    ]
    weight_copies = []
    for h, part in enumerate((mine, other)):
        weight_copies.append(local(gate_hbm.at[0, part, :], wg.at[h]))
        weight_copies.append(local(up_hbm.at[0, part, :], wu.at[h]))
    down_copies = [local(down_hbm.at[0, other, :], wd.at[1]), local(down_hbm.at[0, mine, :], wd.at[0])]

    barrier = pltpu.get_barrier_semaphore()
    for dz in range(nz):
        for r in range(2):
            if dz or r:
                peer = {"expert": ((z + dz) % nz) * 2 + (c if r == 0 else 1 - c)}
                pl.semaphore_signal(barrier, inc=1, device_id=peer, device_id_type=MESH)
    pl.semaphore_signal(barrier, inc=1, device_id=across, device_id_type=MESH)

    diagonal = lax.broadcasted_iota(jnp.int32, (tok, LANES), 0) == lax.broadcasted_iota(
        jnp.int32, (tok, LANES), 1
    )
    named = slots[...]
    expert = lax.shift_right_logical(named, 1)
    target = expert
    for d in range(experts):
        target = jnp.where(expert == d, plan[d], target)
    expert = jnp.where((named & 1) == 0, expert, target)
    gate = gates[...]
    grow_send[...] = jnp.zeros_like(grow_send)
    for e in range(experts):
        grow_send[e, :, :tok] = jnp.sum(jnp.where(expert == e, gate, 0.0), axis=0, keepdims=True)

    pl.semaphore_wait(barrier, experts)

    pieces = tok // ROWS
    cuts = [pl.ds(q * ROWS, ROWS) for q in range(pieces)]

    def piece(h, r, slot, q):
        return rows.at[h, r, slot, cuts[q]], row_sem.at[h, r, slot, q]

    for q in range(pieces):
        for step in (1, -1):
            send(
                tokens.at[cuts[q], mine], *piece(0, 0, z, q),
                {"expert": (z + step) * 2 + c}, (z + step >= 0) & (z + step < nz),
            )
    for h, part in enumerate((mine, other)):
        for q in range(pieces):
            send(tokens.at[cuts[q], part], *piece(h, 1, z, q), partner)
    for dz in range(nz):
        for r in range(2):
            if dz or r:
                peer = ((z + dz) % nz) * 2 + (c if r == 0 else 1 - c)
                send(grow_send.at[peer], grow.at[r, z], g_sem.at[r, z], {"expert": peer})
    grow[0, z] = grow_send[me]

    items = [(hop, q) for hop in range(1, nz) for q in range(pieces)]

    def from_z(hop, q):
        for step in (1, -1):
            origin = z - step * hop
            valid = (origin >= 0) & (origin < nz)
            slot = jnp.clip(origin, 0, nz - 1)
            block, sem = piece(0, 0, slot, q)
            pl.when(valid)(functools.partial(arrived, block, sem))
            if hop < nz - 1:
                send(
                    block, block, sem, {"expert": (z + step) * 2 + c},
                    valid & (z + step >= 0) & (z + step < nz),
                )
            send(block, *piece(1, 0, slot, q), across, valid)
            send(block, *piece(0, 1, slot, q), partner, valid)

    def from_across(hop, q):
        for step in (1, -1):
            origin = z - step * hop
            valid = (origin >= 0) & (origin < nz)
            slot = jnp.clip(origin, 0, nz - 1)
            block, sem = piece(1, 0, slot, q)
            pl.when(valid)(functools.partial(arrived, block, sem))
            send(block, *piece(1, 1, slot, q), partner, valid)

    def from_partner(h):
        for dz in range(nz):
            for q in range(pieces):
                arrived(*piece(h, 1, (z + dz) % nz, q))

    total = 2 * nz * tok
    units = wg.shape[-1]
    tile = 256 if units % 256 == 0 else LANES
    tiles = [pl.ds(t * tile, tile) for t in range(units // tile)]

    def product(h, weights, cols):
        return jnp.dot(
            rows[h].reshape(total, half), weights[h, :, cols], preferred_element_type=f32
        )

    late = 2
    for i, item in enumerate(items):
        from_z(*item)
        if i >= late:
            from_across(*items[i - late])

    for copy in own_copies + weight_copies[:2]:
        copy.wait()
    from_partner(0)
    rest = list(items[-late:])
    for cols in tiles:
        acc[0, :, cols] = product(0, wg, cols)
        acc[1, :, cols] = product(0, wu, cols)
        if rest:
            from_across(*rest.pop(0))
    for item in rest:
        from_across(*item)

    for dz in range(nz):
        for r in range(2):
            if dz or r:
                slot = (z + dz) % nz
                arrived(grow.at[r, slot], g_sem.at[r, slot])
    for r in range(2):
        for i in range(nz):
            column = jnp.sum(jnp.where(diagonal, grow[r, i], 0.0), axis=1, keepdims=True)
            scale[r, i] = jnp.broadcast_to(column, (tok, width))
    for copy in weight_copies[2:]:
        copy.wait()
    from_partner(1)
    for cols in tiles:
        gate_act = acc[0, :, cols] + product(1, wg, cols)
        up_act = acc[1, :, cols] + product(1, wu, cols)
        hid[:, cols] = (gate_act / (1.0 + jnp.exp(-gate_act)) * up_act).astype(bf16)

    for copy in down_copies:
        copy.wait()

    def cross(j):
        arrived(a_recv.at[1, j], a_sem.at[1, j])
        b_send[j] = (keep[1, j] + a_recv[1, j].astype(f32)).astype(bf16)
        send(b_send.at[j], b_recv.at[j], b_sem.at[j], across)

    early = steps - z_first
    sums = [(h, j) for j in range(early, steps) for h in (1, 0)]

    def along_z(h, j):
        n = sums.index((h, j))
        arrived(a_recv.at[h, j], a_sem.at[h, j])
        zc_send[n] = (keep[h, j] + a_recv[h, j].astype(f32)).astype(bf16)
        for d in range(nz - 1):
            peer = (z + d + 1) % nz
            send(zc_send.at[n, peer], zc_recv.at[n, d], zc_sem.at[n, d], {"expert": peer * 2 + c})

    def after(h, j):
        if j >= early:
            along_z(h, j)
        elif h:
            cross(j)

    order = [(1, j) for j in range(min(2, early))] + sums
    for j in range(early):
        if j + 2 < early:
            order.append((1, j + 2))
        order.append((0, j))
    for i, (h, j) in enumerate(order):
        down = lax.dot_general(
            hid[...], wd[h, pl.ds(j * width, width), :], (((1,), (1,)), ((), ())),
            preferred_element_type=f32,
        )
        down = down.reshape(2, nz, tok, width) * scale[...]
        a_send[h, j] = down[1].astype(bf16)
        keep[h, j] = down[0]
        send(a_send.at[h, j], a_recv.at[h, j], a_sem.at[h, j], partner)
        if i:
            after(*order[i - 1])
    after(*order[-1])

    out_copies = []

    def finish(j):
        value = keep[0, j, z] + a_recv[0, j, z].astype(f32) + b_recv[j, z].astype(f32)
        for d in range(nz - 1):
            arrived(c_recv.at[j, d], c_sem.at[j, d])
        for d in range(nz - 1):
            value = value + c_recv[j, d].astype(f32)
        d_send[j] = value.astype(bf16)
        cols = pl.ds(pl.multiple_of(x * half + j * width, LANES), width)
        send(d_send.at[j], out.at[:, cols], d_sem.at[j], across)
        out_copies.append(local(d_send.at[j], out.at[:, cols]))

    def exchange(h, j):
        n = sums.index((h, j))
        value = keep[h, j, z] + a_recv[h, j, z].astype(f32)
        for d in range(nz - 1):
            arrived(zc_recv.at[n, d], zc_sem.at[n, d])
        for d in range(nz - 1):
            value = value + zc_recv[n, d].astype(f32)
        e_send[n] = value.astype(bf16)
        send(e_send.at[n], e_recv.at[n ^ 1], e_sem.at[n ^ 1], across)

    def close(h, j):
        n = sums.index((h, j))
        arrived(e_recv.at[n], e_sem.at[n])
        e_out[n] = (e_send[n].astype(f32) + e_recv[n].astype(f32)).astype(bf16)
        start = (x if h == 0 else 1 - x) * half + j * width
        out_copies.append(local(e_out.at[n], out.at[:, pl.ds(pl.multiple_of(start, LANES), width)]))

    for j in range(early + LAG):
        if j < early:
            arrived(a_recv.at[0, j], a_sem.at[0, j])
            arrived(b_recv.at[j], b_sem.at[j])
            c_send[j] = (keep[0, j] + a_recv[0, j].astype(f32) + b_recv[j].astype(f32)).astype(bf16)
            for d in range(nz - 1):
                peer = (z + d + 1) % nz
                send(
                    c_send.at[j, peer], c_recv.at[j, d], c_sem.at[j, d], {"expert": peer * 2 + c}
                )
        if j == min(z_first + 1, early - 1):
            for pair in sums:
                exchange(*pair)
        if j >= LAG:
            finish(j - LAG)
        if j == early:
            for pair in sums:
                close(*pair)

    for j in range(early):
        cols = pl.ds(pl.multiple_of((1 - x) * half + j * width, LANES), width)
        arrived(out.at[:, cols], d_sem.at[j])
    for copy in out_copies:
        copy.wait()
    for when, copy in pending:
        if when is None:
            copy.wait_send()
        else:
            pl.when(when)(copy.wait_send)


def fused_body(tokens, gates, slots, plan, gate_proj, up_proj, down_proj):
    f32, bf16 = jnp.float32, jnp.bfloat16
    nz = lax.axis_size("expert") // 2
    tok, model = tokens.shape
    half = model // 2
    units = gate_proj.shape[2]
    width = 256 if half % 256 == 0 else LANES
    steps = half // width
    z_first = min(Z_FIRST, steps - 1)
    extra = max(1, 2 * z_first)
    dma = pltpu.SemaphoreType.DMA
    vmem, anywhere = pl.BlockSpec(memory_space=pltpu.VMEM), pl.BlockSpec(memory_space=pl.ANY)
    sends = extra * nz + 2 * nz + (4 + 8 * nz) * (tok // ROWS) + steps * (3 + nz)
    return pl.pallas_call(
        functools.partial(kernel, nz, steps, width, z_first),
        out_shape=jax.ShapeDtypeStruct((tok, model), bf16),
        in_specs=[
            anywhere, vmem, vmem, pl.BlockSpec(memory_space=pltpu.SMEM),
            anywhere, anywhere, anywhere,
        ],
        out_specs=anywhere,
        scratch_shapes=[
            pltpu.VMEM((2, 2, nz, tok, half), bf16),
            pltpu.VMEM((2, half, units), bf16),
            pltpu.VMEM((2, half, units), bf16),
            pltpu.VMEM((2, half, units), bf16),
            pltpu.VMEM((2, 2 * nz * tok, units), f32),
            pltpu.VMEM((2 * nz * tok, units), bf16),
            pltpu.VMEM((2, nz, tok, width), f32),
            pltpu.VMEM((2 * nz, 1, LANES), f32),
            pltpu.VMEM((2, nz, 1, LANES), f32),
            pltpu.VMEM((2, steps, nz, tok, width), f32),
            pltpu.VMEM((2, steps, nz, tok, width), bf16),
            pltpu.VMEM((2, steps, nz, tok, width), bf16),
            pltpu.VMEM((steps, nz, tok, width), bf16),
            pltpu.VMEM((steps, nz, tok, width), bf16),
            pltpu.VMEM((steps, nz, tok, width), bf16),
            pltpu.VMEM((steps, nz - 1, tok, width), bf16),
            pltpu.VMEM((steps, tok, width), bf16),
            pltpu.VMEM((extra, nz, tok, width), bf16),
            pltpu.VMEM((extra, nz - 1, tok, width), bf16),
            pltpu.VMEM((extra, tok, width), bf16),
            pltpu.VMEM((extra, tok, width), bf16),
            pltpu.VMEM((extra, tok, width), bf16),
            dma((sends,)),
            dma((8 + steps + extra,)),
            dma((2, 2, nz, tok // ROWS)),
            dma((2, nz)),
            dma((2, steps)),
            dma((steps,)),
            dma((steps, nz - 1)),
            dma((steps,)),
            dma((extra, nz - 1)),
            dma((extra,)),
        ],
        compiler_params=pltpu.CompilerParams(collective_id=0, has_side_effects=True),
    )(tokens, gates.T, slots.T, plan, gate_proj, up_proj, down_proj)


def body(tokens, gates, slots, plan, gate_proj, up_proj, down_proj):
    experts, attn = lax.axis_size("expert"), lax.axis_size("attn")
    tok, model = tokens.shape
    fits = (
        attn == 2 and experts % 2 == 0 and experts > 2
        and tok % ROWS == 0 and tok <= LANES
        and model % (2 * LANES) == 0 and gate_proj.shape[0] == 1
        and gate_proj.shape[2] % LANES == 0
    )
    chosen = fused_body if fits else dense_body
    return chosen(tokens, gates, slots, plan, gate_proj, up_proj, down_proj)


def solution(mesh):
    return jax.shard_map(
        body,
        mesh=mesh,
        in_specs=(
            P(("groups", "expert"), None),
            P(("groups", "expert"), None),
            P(("groups", "expert"), None),
            P("groups"),
            P("expert", None, "attn"),
            P("expert", None, "attn"),
            P("expert", None, "attn"),
        ),
        out_specs=P(("groups", "expert"), None),
        check_vma=False,
    )
```

```python
import functools

import jax
import jax.numpy as jnp
from jax import lax
from jax.experimental import pallas as pl
from jax.experimental.pallas import tpu as pltpu
from jax.sharding import PartitionSpec as P

MESH = pl.DeviceIdType.MESH
LANES = 128
LAG = 5
ROWS = 16
Z_FIRST = 2


def combined_gates(gates, slots, plan, experts):
    choice = slots // 2
    expert = jnp.where(slots % 2 == 0, choice, plan[choice])
    ids = jnp.arange(experts, dtype=jnp.int32)
    return jnp.sum(jnp.where(expert[:, :, None] == ids, gates[:, :, None], 0.0), axis=1)


def dense_body(tokens, gates, slots, plan, gate_proj, up_proj, down_proj):
    experts = lax.axis_size("expert")
    weight = combined_gates(gates, slots, plan, experts)
    everyone = lax.all_gather(tokens, "expert", axis=0, tiled=True)
    weights = lax.all_to_all(weight, "expert", split_axis=1, concat_axis=0, tiled=True)
    gate_act = jnp.dot(everyone, gate_proj[0], preferred_element_type=jnp.float32)
    up_act = jnp.dot(everyone, up_proj[0], preferred_element_type=jnp.float32)
    hidden = (jax.nn.silu(gate_act) * up_act).astype(jnp.bfloat16)
    down = jnp.einsum("rf,df->rd", hidden, down_proj[0], preferred_element_type=jnp.float32)
    part = (down * weights).astype(jnp.bfloat16)
    part = lax.psum_scatter(part, "expert", scatter_dimension=0, tiled=True)
    return lax.psum(part, "attn")


def kernel(
    nz, steps, width, z_first,
    tokens, gates, slots, plan, gate_hbm, up_hbm, down_hbm,
    out,
    rows, wg, wu, wd, acc, hid, scale, grow_send, grow,
    keep, a_send, a_recv, b_send, b_recv, c_send, c_recv, d_send,
    zc_send, zc_recv, e_send, e_recv, e_out,
    send_sem, local_sem, row_sem, g_sem, a_sem, b_sem, c_sem, d_sem, zc_sem, e_sem,
):
    f32, bf16 = jnp.float32, jnp.bfloat16
    experts = 2 * nz
    me = lax.axis_index("expert")
    x = lax.axis_index("attn")
    z, c = me // 2, me % 2
    half = rows.shape[-1]
    tok = rows.shape[-2]
    mine = pl.ds(pl.multiple_of(x * half, LANES), half)
    other = pl.ds(pl.multiple_of((1 - x) * half, LANES), half)
    partner = {"expert": z * 2 + (1 - c)}
    across = {"attn": 1 - x}

    counts = {"send": 0, "local": 0}
    pending = []

    def local(src, dst):
        copy = pltpu.make_async_copy(src, dst, local_sem.at[counts["local"]])
        counts["local"] += 1
        copy.start()
        return copy

    def send(src, dst, sem, device, when=None):
        copy = pltpu.make_async_remote_copy(
            src_ref=src, dst_ref=dst, send_sem=send_sem.at[counts["send"]], recv_sem=sem,
            device_id=device, device_id_type=MESH,
        )
        counts["send"] += 1
        if when is None:
            copy.start()
        else:
            pl.when(when)(copy.start)
        pending.append((when, copy))

    def arrived(dst, sem):
        pltpu.make_async_remote_copy(
            src_ref=dst, dst_ref=dst, send_sem=send_sem.at[0], recv_sem=sem,
            device_id=partner, device_id_type=MESH,
        ).wait_recv()

    own_copies = [
        local(tokens.at[:, mine], rows.at[0, 0, z]),
        local(tokens.at[:, other], rows.at[1, 0, z]),
    ]
    weight_copies = []
    for h, part in enumerate((mine, other)):
        weight_copies.append(local(gate_hbm.at[0, part, :], wg.at[h]))
        weight_copies.append(local(up_hbm.at[0, part, :], wu.at[h]))
    down_copies = [local(down_hbm.at[0, other, :], wd.at[1]), local(down_hbm.at[0, mine, :], wd.at[0])]

    barrier = pltpu.get_barrier_semaphore()
    for dz in range(nz):
        for r in range(2):
            if dz or r:
                peer = {"expert": ((z + dz) % nz) * 2 + (c if r == 0 else 1 - c)}
                pl.semaphore_signal(barrier, inc=1, device_id=peer, device_id_type=MESH)
    pl.semaphore_signal(barrier, inc=1, device_id=across, device_id_type=MESH)

    diagonal = lax.broadcasted_iota(jnp.int32, (tok, LANES), 0) == lax.broadcasted_iota(
        jnp.int32, (tok, LANES), 1
    )
    named = slots[...]
    expert = lax.shift_right_logical(named, 1)
    target = expert
    for d in range(experts):
        target = jnp.where(expert == d, plan[d], target)
    expert = jnp.where((named & 1) == 0, expert, target)
    gate = gates[...]
    grow_send[...] = jnp.zeros_like(grow_send)
    for e in range(experts):
        grow_send[e, :, :tok] = jnp.sum(jnp.where(expert == e, gate, 0.0), axis=0, keepdims=True)

    pl.semaphore_wait(barrier, experts)

    pieces = tok // ROWS
    cuts = [pl.ds(q * ROWS, ROWS) for q in range(pieces)]

    def piece(h, r, slot, q):
        return rows.at[h, r, slot, cuts[q]], row_sem.at[h, r, slot, q]

    for q in range(pieces):
        for step in (1, -1):
            send(
                tokens.at[cuts[q], mine], *piece(0, 0, z, q),
                {"expert": (z + step) * 2 + c}, (z + step >= 0) & (z + step < nz),
            )
    for h, part in enumerate((mine, other)):
        for q in range(pieces):
            send(tokens.at[cuts[q], part], *piece(h, 1, z, q), partner)
    for dz in range(nz):
        for r in range(2):
            if dz or r:
                peer = ((z + dz) % nz) * 2 + (c if r == 0 else 1 - c)
                send(grow_send.at[peer], grow.at[r, z], g_sem.at[r, z], {"expert": peer})
    grow[0, z] = grow_send[me]

    items = [(hop, q) for hop in range(1, nz) for q in range(pieces)]

    def from_z(hop, q):
        for step in (1, -1):
            origin = z - step * hop
            valid = (origin >= 0) & (origin < nz)
            slot = jnp.clip(origin, 0, nz - 1)
            block, sem = piece(0, 0, slot, q)
            pl.when(valid)(functools.partial(arrived, block, sem))
            if hop < nz - 1:
                send(
                    block, block, sem, {"expert": (z + step) * 2 + c},
                    valid & (z + step >= 0) & (z + step < nz),
                )
            send(block, *piece(1, 0, slot, q), across, valid)
            send(block, *piece(0, 1, slot, q), partner, valid)

    def from_across(hop, q):
        for step in (1, -1):
            origin = z - step * hop
            valid = (origin >= 0) & (origin < nz)
            slot = jnp.clip(origin, 0, nz - 1)
            block, sem = piece(1, 0, slot, q)
            pl.when(valid)(functools.partial(arrived, block, sem))
            send(block, *piece(1, 1, slot, q), partner, valid)

    def from_partner(h):
        for dz in range(nz):
            for q in range(pieces):
                arrived(*piece(h, 1, (z + dz) % nz, q))

    total = 2 * nz * tok
    units = wg.shape[-1]
    tile = 256 if units % 256 == 0 else LANES
    tiles = [pl.ds(t * tile, tile) for t in range(units // tile)]

    def product(h, weights, cols):
        return jnp.dot(
            rows[h].reshape(total, half), weights[h, :, cols], preferred_element_type=f32
        )

    late = 3
    for i, item in enumerate(items):
        from_z(*item)
        if i >= late:
            from_across(*items[i - late])

    for copy in own_copies + weight_copies[:2]:
        copy.wait()
    from_partner(0)
    rest = list(items[-late:])
    for cols in tiles:
        acc[0, :, cols] = product(0, wg, cols)
        acc[1, :, cols] = product(0, wu, cols)
        if rest:
            from_across(*rest.pop(0))
    for item in rest:
        from_across(*item)

    for dz in range(nz):
        for r in range(2):
            if dz or r:
                slot = (z + dz) % nz
                arrived(grow.at[r, slot], g_sem.at[r, slot])
    for r in range(2):
        for i in range(nz):
            column = jnp.sum(jnp.where(diagonal, grow[r, i], 0.0), axis=1, keepdims=True)
            scale[r, i] = jnp.broadcast_to(column, (tok, width))
    for copy in weight_copies[2:]:
        copy.wait()
    from_partner(1)
    for cols in tiles:
        gate_act = acc[0, :, cols] + product(1, wg, cols)
        up_act = acc[1, :, cols] + product(1, wu, cols)
        hid[:, cols] = (gate_act / (1.0 + jnp.exp(-gate_act)) * up_act).astype(bf16)

    for copy in down_copies:
        copy.wait()

    def cross(j):
        arrived(a_recv.at[1, j], a_sem.at[1, j])
        b_send[j] = (keep[1, j] + a_recv[1, j].astype(f32)).astype(bf16)
        send(b_send.at[j], b_recv.at[j], b_sem.at[j], across)

    early = steps - z_first
    sums = [(h, j) for j in range(early, steps) for h in (1, 0)]

    def along_z(h, j):
        n = sums.index((h, j))
        arrived(a_recv.at[h, j], a_sem.at[h, j])
        zc_send[n] = (keep[h, j] + a_recv[h, j].astype(f32)).astype(bf16)
        for d in range(nz - 1):
            peer = (z + d + 1) % nz
            send(zc_send.at[n, peer], zc_recv.at[n, d], zc_sem.at[n, d], {"expert": peer * 2 + c})

    def after(h, j):
        if j >= early:
            along_z(h, j)
        elif h:
            cross(j)

    order = [(1, j) for j in range(min(2, early))] + sums
    for j in range(early):
        if j + 2 < early:
            order.append((1, j + 2))
        order.append((0, j))
    for i, (h, j) in enumerate(order):
        down = lax.dot_general(
            hid[...], wd[h, pl.ds(j * width, width), :], (((1,), (1,)), ((), ())),
            preferred_element_type=f32,
        )
        down = down.reshape(2, nz, tok, width) * scale[...]
        a_send[h, j] = down[1].astype(bf16)
        keep[h, j] = down[0]
        send(a_send.at[h, j], a_recv.at[h, j], a_sem.at[h, j], partner)
        if i:
            after(*order[i - 1])
    after(*order[-1])

    out_copies = []

    def finish(j):
        value = keep[0, j, z] + a_recv[0, j, z].astype(f32) + b_recv[j, z].astype(f32)
        for d in range(nz - 1):
            arrived(c_recv.at[j, d], c_sem.at[j, d])
        for d in range(nz - 1):
            value = value + c_recv[j, d].astype(f32)
        d_send[j] = value.astype(bf16)
        cols = pl.ds(pl.multiple_of(x * half + j * width, LANES), width)
        send(d_send.at[j], out.at[:, cols], d_sem.at[j], across)
        out_copies.append(local(d_send.at[j], out.at[:, cols]))

    def exchange(h, j):
        n = sums.index((h, j))
        value = keep[h, j, z] + a_recv[h, j, z].astype(f32)
        for d in range(nz - 1):
            arrived(zc_recv.at[n, d], zc_sem.at[n, d])
        for d in range(nz - 1):
            value = value + zc_recv[n, d].astype(f32)
        e_send[n] = value.astype(bf16)
        send(e_send.at[n], e_recv.at[n ^ 1], e_sem.at[n ^ 1], across)

    def close(h, j):
        n = sums.index((h, j))
        arrived(e_recv.at[n], e_sem.at[n])
        e_out[n] = (e_send[n].astype(f32) + e_recv[n].astype(f32)).astype(bf16)
        start = (x if h == 0 else 1 - x) * half + j * width
        out_copies.append(local(e_out.at[n], out.at[:, pl.ds(pl.multiple_of(start, LANES), width)]))

    for j in range(early + LAG):
        if j < early:
            arrived(a_recv.at[0, j], a_sem.at[0, j])
            arrived(b_recv.at[j], b_sem.at[j])
            c_send[j] = (keep[0, j] + a_recv[0, j].astype(f32) + b_recv[j].astype(f32)).astype(bf16)
            for d in range(nz - 1):
                peer = (z + d + 1) % nz
                send(
                    c_send.at[j, peer], c_recv.at[j, d], c_sem.at[j, d], {"expert": peer * 2 + c}
                )
        if j == min(z_first + 1, early - 1):
            for pair in sums:
                exchange(*pair)
        if j >= LAG:
            finish(j - LAG)
        if j == early:
            for pair in sums:
                close(*pair)

    for j in range(early):
        cols = pl.ds(pl.multiple_of((1 - x) * half + j * width, LANES), width)
        arrived(out.at[:, cols], d_sem.at[j])
    for copy in out_copies:
        copy.wait()
    for when, copy in pending:
        if when is None:
            copy.wait_send()
        else:
            pl.when(when)(copy.wait_send)


def fused_body(tokens, gates, slots, plan, gate_proj, up_proj, down_proj):
    f32, bf16 = jnp.float32, jnp.bfloat16
    nz = lax.axis_size("expert") // 2
    tok, model = tokens.shape
    half = model // 2
    units = gate_proj.shape[2]
    width = 256 if half % 256 == 0 else LANES
    steps = half // width
    z_first = min(Z_FIRST, steps - 1)
    extra = max(1, 2 * z_first)
    dma = pltpu.SemaphoreType.DMA
    vmem, anywhere = pl.BlockSpec(memory_space=pltpu.VMEM), pl.BlockSpec(memory_space=pl.ANY)
    sends = extra * nz + 2 * nz + (4 + 8 * nz) * (tok // ROWS) + steps * (3 + nz)
    return pl.pallas_call(
        functools.partial(kernel, nz, steps, width, z_first),
        out_shape=jax.ShapeDtypeStruct((tok, model), bf16),
        in_specs=[
            anywhere, vmem, vmem, pl.BlockSpec(memory_space=pltpu.SMEM),
            anywhere, anywhere, anywhere,
        ],
        out_specs=anywhere,
        scratch_shapes=[
            pltpu.VMEM((2, 2, nz, tok, half), bf16),
            pltpu.VMEM((2, half, units), bf16),
            pltpu.VMEM((2, half, units), bf16),
            pltpu.VMEM((2, half, units), bf16),
            pltpu.VMEM((2, 2 * nz * tok, units), f32),
            pltpu.VMEM((2 * nz * tok, units), bf16),
            pltpu.VMEM((2, nz, tok, width), f32),
            pltpu.VMEM((2 * nz, 1, LANES), f32),
            pltpu.VMEM((2, nz, 1, LANES), f32),
            pltpu.VMEM((2, steps, nz, tok, width), f32),
            pltpu.VMEM((2, steps, nz, tok, width), bf16),
            pltpu.VMEM((2, steps, nz, tok, width), bf16),
            pltpu.VMEM((steps, nz, tok, width), bf16),
            pltpu.VMEM((steps, nz, tok, width), bf16),
            pltpu.VMEM((steps, nz, tok, width), bf16),
            pltpu.VMEM((steps, nz - 1, tok, width), bf16),
            pltpu.VMEM((steps, tok, width), bf16),
            pltpu.VMEM((extra, nz, tok, width), bf16),
            pltpu.VMEM((extra, nz - 1, tok, width), bf16),
            pltpu.VMEM((extra, tok, width), bf16),
            pltpu.VMEM((extra, tok, width), bf16),
            pltpu.VMEM((extra, tok, width), bf16),
            dma((sends,)),
            dma((8 + steps + extra,)),
            dma((2, 2, nz, tok // ROWS)),
            dma((2, nz)),
            dma((2, steps)),
            dma((steps,)),
            dma((steps, nz - 1)),
            dma((steps,)),
            dma((extra, nz - 1)),
            dma((extra,)),
        ],
        compiler_params=pltpu.CompilerParams(collective_id=0, has_side_effects=True),
    )(tokens, gates.T, slots.T, plan, gate_proj, up_proj, down_proj)


def body(tokens, gates, slots, plan, gate_proj, up_proj, down_proj):
    experts, attn = lax.axis_size("expert"), lax.axis_size("attn")
    tok, model = tokens.shape
    fits = (
        attn == 2 and experts % 2 == 0 and experts > 2
        and tok % ROWS == 0 and tok <= LANES
        and model % (2 * LANES) == 0 and gate_proj.shape[0] == 1
        and gate_proj.shape[2] % LANES == 0
    )
    chosen = fused_body if fits else dense_body
    return chosen(tokens, gates, slots, plan, gate_proj, up_proj, down_proj)


def solution(mesh):
    return jax.shard_map(
        body,
        mesh=mesh,
        in_specs=(
            P(("groups", "expert"), None),
            P(("groups", "expert"), None),
            P(("groups", "expert"), None),
            P("groups"),
            P("expert", None, "attn"),
            P("expert", None, "attn"),
            P("expert", None, "attn"),
        ),
        out_specs=P(("groups", "expert"), None),
        check_vma=False,
    )
```
